256 devices in a mesh: tile: 128 (over z, x_hi, y, core), real: 2 (over x_lo).
Axes of the slice: x: 4 (x_hi: 2, x_lo: 2; x = x_hi * 2 + x_lo), y: 4, z: 8, core: 2. Of those that a mesh axis runs over, the one named last changes fastest.
Arguments:
- voltage: float32 [64, 131072], P('real', 'tile'), parts along dimension 0, may hold values from -4 to 4
- recovery: float32 [64, 131072], P('real', 'tile'), parts along dimension 0, may hold values from -3 to 3
- increments: float32 [10, 64, 131072], P(None, 'real', 'tile'), parts along dimension 1, may hold values from -6 to 6
- band_weight: bfloat16 [131072, 3072], P('tile'), may hold values from -0.125 to 0.125
- time_scale: float32 [131072], P('tile'), may hold values from 0.05 to 0.5
- tract_in: bfloat16 [4, 131072, 256], P(None, 'tile'), may hold values from -0.375 to 0.375
- tract_out: bfloat16 [4, 131072, 256], P(None, 'tile'), may hold values from -0.1875 to 0.1875
- matching_masks: int32 [4], replicated, may hold values from 1 to 127, as said below
- tract_on: int32 [128, 4], P('tile'), may hold values 0 or 1
Outputs:
- voltage_end: float32 [64, 131072], P('real', 'tile'), parts along dimension 0
- recovery_end: float32 [64, 131072], P('real', 'tile'), parts along dimension 0
The draws below stay inside these ranges and needn't reach their ends.
There are 2 independent parts, one for each index of `real`. The reference program is written for one: setup_inputs(seed, part) draws one part's arguments, and reference() takes and returns one part's arrays. A program takes and returns all parts, laid end to end along the dimension named above; an argument that names none is the same for every part. Nothing has to cross between parts.
Inputs may be any that keep to these rules, and one draw needn't show every extreme that they name: `matching_masks`: the 4 masks are distinct.
All inputs are finite; a program needn't handle non-finite values. No bound on the sum of `tract_on` on one device may be relied on, other than what follows from the above.
Results may differ from the reference program's by a relative error of at most 0.0013.
Values may be sent and summed in bfloat16 or wider, within the bound.
No kernel may reach another device: no remote copies, remote signals or barrier semaphores. Data moves between devices by JAX's collectives and lax.ppermute only.
A program may use at most 64 MiB of HBM per device.

```python
import math
import jax
import jax.numpy as jnp
from jax import lax

R = 32
TILE_V = 1024
HW = 1024
RANK = 256
MATCH = 4
STEPS = 10
TILES = 128
VERTS = 131072


def draw_matching_masks(key, part):
    return (jax.random.permutation(key, TILES - 1)[:MATCH] + 1).astype(jnp.int32)


def with_ends(result, stream_key, low, high):
    shape = result.shape
    spot = [jax.random.randint(jax.random.fold_in(stream_key, axis), (), 0, shape[axis]) for axis in range(len(shape))]
    result = result.at[tuple(spot)].set(low)
    longest = shape.index(max(shape))
    spot[longest] = (spot[longest] + 1) % shape[longest]
    return result.at[tuple(spot)].set(high)


def block_scale(own_key, extent, split, least, largest):
    def one(dim, shards_of):
        heights = jax.random.uniform(jax.random.fold_in(jax.random.fold_in(own_key, 6), dim), (shards_of,), jnp.float32, least / len(split), largest / len(split))
        return jnp.repeat(jnp.exp(heights), extent[dim] // shards_of).reshape((-1,) + (1,) * (len(extent) - dim - 1))

    level = one(*split[0])
    for cut in split[1:]:
        level = level * one(*cut)
    return level


def bell_draw(stream_key, shape, width, bound, shards=(), held_as=jnp.bfloat16):
    values = width * jax.random.normal(stream_key, shape, jnp.float32)
    if shards:
        values = values * block_scale(stream_key, shape, shards, -0.22, 0.18)
    return jnp.clip(values, -bound, bound).astype(held_as)


def setup_inputs(seed: int = 0, part: int = 0) -> dict:
    key_list = jax.random.split(jax.random.key(seed), 10)
    part_keys = jax.random.split(jax.random.fold_in(key_list[9], part), 10)
    return {
        "voltage": bell_draw(part_keys[0], (R, VERTS), 1.0, 4.0, ((1, 128),), jnp.float32),
        "recovery": bell_draw(part_keys[1], (R, VERTS), 0.5, 3.0, ((1, 128),), jnp.float32),
        "increments": bell_draw(part_keys[2], (STEPS, R, VERTS), 1.0, 6.0, ((2, 128),), jnp.float32),
        "band_weight": bell_draw(key_list[3], (VERTS, TILE_V + 2 * HW), (2 * HW) ** -0.5, 0.125, ((0, 128),)),
        "time_scale": jnp.clip(jnp.exp(math.log(0.5) - 2.3025851 * jax.random.uniform(key_list[4], (VERTS,), jnp.float32) ** block_scale(key_list[4], (VERTS,), ((0, 128),), -0.2, 0.2)), 0.05, 0.5),
        "tract_in": bell_draw(key_list[5], (MATCH, VERTS, RANK), RANK ** -0.5, 0.375, ((1, 128),)),
        "tract_out": bell_draw(key_list[6], (MATCH, VERTS, RANK), TILE_V ** -0.5, 0.1875, ((1, 128),)),
        "matching_masks": draw_matching_masks(jax.random.fold_in(key_list[9], 71), part),
        "tract_on": with_ends((jax.random.randint(key_list[8], (TILES, MATCH), 0, 4) < 3).astype(jnp.int32), jax.random.fold_in(key_list[8], 1), 0, 1),
    }


time_step = 0.1
noise_gain = 0.5
shift_a = 0.7
damp_b = 0.8
drive_level = 0.5
band_gain = 1.0
tract_gain = 0.5

def reference(voltage, recovery, increments, band_weight, time_scale, tract_in, tract_out, matching_masks, tract_on):
    window_width = TILE_V + 2 * HW
    row_index = jnp.arange(TILE_V, dtype=jnp.int32)[:, None]
    col_index = jnp.arange(window_width, dtype=jnp.int32)[None, :]
    inband = (col_index - row_index >= 0) & (col_index - row_index <= 2 * HW)
    banded = jnp.where(inband[None], band_weight.reshape(TILES, TILE_V, window_width), jnp.zeros((), jnp.bfloat16))
    partner = jnp.bitwise_xor(jnp.arange(TILES, dtype=jnp.int32)[:, None], matching_masks[None, :])
    gate_float = tract_on.astype(jnp.float32)
    in_tiles = tract_in.reshape(MATCH, TILES, TILE_V, RANK).astype(jnp.float32)
    out_tiles = tract_out.reshape(MATCH, TILES, TILE_V, RANK).astype(jnp.float32)
    match_index = jnp.arange(MATCH, dtype=jnp.int32)[None, :]

    def advance(state_pair, kick_now):
        voltage_now, recovery_now = state_pair
        rounded = voltage_now.astype(jnp.bfloat16)
        padded = jnp.pad(rounded, ((0, 0), (HW, HW)))

        def tile_band(tile_at):
            window = lax.dynamic_slice_in_dim(padded, (tile_at * TILE_V).astype(jnp.int32), window_width, 1)
            return jnp.dot(window, banded[tile_at].T, preferred_element_type=jnp.float32)
        band_drive = lax.map(tile_band, jnp.arange(TILES, dtype=jnp.int32))
        band_drive = band_drive.transpose(1, 0, 2).reshape(R, VERTS)
        projected = jnp.einsum('rtv,mtvk->tmrk', rounded.reshape(R, TILES, TILE_V).astype(jnp.float32), out_tiles).astype(jnp.bfloat16)
        received = projected[partner, match_index].astype(jnp.float32) * gate_float[:, :, None, None]
        tract_drive = jnp.einsum('tmrk,mtvk->rtv', received, in_tiles).reshape(R, VERTS)
        total_drive = band_gain * band_drive + tract_gain * tract_drive + drive_level
        voltage_new = voltage_now + time_step * (voltage_now - voltage_now ** 3 / 3.0 - recovery_now + total_drive) + noise_gain * math.sqrt(time_step) * kick_now
        recovery_new = recovery_now + time_step * time_scale[None, :] * (voltage_now + shift_a - damp_b * recovery_now)
        return ((voltage_new, recovery_new), None)
    (voltage_end, recovery_end), unused = lax.scan(advance, (voltage, recovery), increments)
    return (voltage_end, recovery_end)
```

```python
import functools
import math

import jax
import jax.numpy as jnp
from jax import lax
from jax.experimental import pallas as pl
from jax.experimental.pallas import tpu as pltpu
from jax.sharding import PartitionSpec as P


TILE_V = 1024
HW = 1024
BLOCK = 256
MATCH = 4
BASIS = (1, 2, 6, 8, 16, 48, 112)

time_step = 0.1
noise_gain = 0.5
shift_a = 0.7
damp_b = 0.8
drive_level = 0.5
band_gain = 1.0
tract_gain = 0.5

VMEM = pl.BlockSpec(memory_space=pltpu.VMEM)
PARAMS = pltpu.CompilerParams(vmem_limit_bytes=10 << 20)


def basis_rows(basis, bits):
    rows = [[basis[j] >> i & 1 for j in range(bits)] + [int(i == j) for j in range(bits)] for i in range(bits)]
    for col in range(bits):
        pivot = next(r for r in range(col, bits) if rows[r][col])
        rows[col], rows[pivot] = rows[pivot], rows[col]
        for r in range(bits):
            if r != col and rows[r][col]:
                rows[r] = [a ^ b for a, b in zip(rows[r], rows[col])]
    return [[i for i in range(bits) if rows[j][bits + i]] for j in range(bits)]


def nt(left, right):
    return lax.dot_general(left, right, (((1,), (1,)), ((), ())), preferred_element_type=jnp.float32)


def project(vb, tract_out_ref, packed_ref):
    for m in range(MATCH):
        packed_ref[m] = jnp.dot(vb, tract_out_ref[m], preferred_element_type=jnp.float32).astype(jnp.bfloat16)


def first_kernel(v_ref, tract_out_ref, packed_ref):
    vb = v_ref[...].astype(jnp.bfloat16)
    project(vb, tract_out_ref, packed_ref)
    for j in range(HW // BLOCK):
        packed_ref[MATCH + j] = vb[:, j * BLOCK : (j + 1) * BLOCK]


def center_kernel(packed_ref, weight_ref, out_ref):
    vb = jnp.concatenate([packed_ref[MATCH + j] for j in range(TILE_V // BLOCK)], axis=1)
    for i in range(TILE_V // BLOCK):
        rows = slice(i * BLOCK, (i + 1) * BLOCK)
        out_ref[:, rows] = nt(vb, weight_ref[rows, HW : HW + TILE_V])


def sides_kernel(
    n, odd_ref, near_ref, far_ref, center_ref, weight_ref, v_ref, w_ref, scale_ref, kick_ref, base_ref, w_out
):
    odd = odd_ref[...] > 0.5
    left, right = [], []
    for j in range(HW // BLOCK):
        near, far = near_ref[MATCH + j].astype(jnp.float32), far_ref[j].astype(jnp.float32)
        left.append(jnp.where(odd, near, far).astype(jnp.bfloat16))
        right.append(jnp.where(odd, far, near).astype(jnp.bfloat16))
    row = lax.broadcasted_iota(jnp.int32, (BLOCK, BLOCK), 0)
    col = lax.broadcasted_iota(jnp.int32, (BLOCK, BLOCK), 1)

    def weights(i, column, keep=None):
        block = weight_ref[i * BLOCK : (i + 1) * BLOCK, column : column + BLOCK]
        if keep is None:
            return block
        return jnp.where(keep, block.astype(jnp.float32), 0.0).astype(jnp.bfloat16)

    for i in range(TILE_V // BLOCK):
        cols = slice(i * BLOCK, (i + 1) * BLOCK)
        band = center_ref[:, cols]
        for j in range(i, HW // BLOCK):
            band += nt(left[j], weights(i, j * BLOCK, col >= row if j == i else None))
        for j in range(i + 1):
            band += nt(right[j], weights(i, HW + TILE_V + j * BLOCK, col <= row if j == i else None))
        v, w = v_ref[:, cols], w_ref[:, cols]
        rate = v - v * v * v / 3.0 - w + band_gain * band + drive_level
        base_ref[:, cols] = v + time_step * rate + noise_gain * math.sqrt(time_step) * kick_ref[n, :, cols]
        w_out[:, cols] = w + time_step * scale_ref[:, cols] * (v + shift_a - damp_b * w)


def update_kernel(received_ref, tract_in_ref, base_ref, tract_out_ref, v_out, packed_ref):
    received = jnp.concatenate([received_ref[m] for m in range(MATCH)], axis=1)
    rounded = []
    for i in range(TILE_V // BLOCK):
        cols = slice(i * BLOCK, (i + 1) * BLOCK)
        tract = jnp.dot(received, tract_in_ref[:, cols], preferred_element_type=jnp.float32)
        v_new = base_ref[:, cols] + time_step * tract_gain * tract
        v_out[:, cols] = v_new
        rounded.append(v_new.astype(jnp.bfloat16))
        packed_ref[MATCH + i] = rounded[i]
    project(jnp.concatenate(rounded, axis=1), tract_out_ref, packed_ref)


def per_device(
    voltage, recovery, increments, band_weight, time_scale, tract_in, tract_out, matching_masks, tract_on
):
    count = lax.axis_size("tile")
    bits = count.bit_length() - 1
    rows = voltage.shape[0]
    rank = tract_out.shape[2]
    parities = basis_rows(BASIS, bits)
    odd = jnp.full((rows, BLOCK), jnp.bitwise_and(lax.axis_index("tile"), 1), jnp.float32)
    far_route = [(i, i + 1) for i in range(1, count - 1, 2)] + [(i + 1, i) for i in range(1, count - 1, 2)]

    def pick(j, arrived, kept):
        folded = sum(jnp.right_shift(matching_masks, b) for b in parities[j])
        chosen = jnp.bitwise_and(folded, 1) == 1
        return jnp.where(chosen[:, None, None], arrived, kept)

    def swap(block, mask):
        return lax.ppermute(block, "tile", [(i, i ^ mask) for i in range(count)])

    state = jax.ShapeDtypeStruct(voltage.shape, jnp.float32)
    packed = jax.ShapeDtypeStruct((MATCH + HW // BLOCK, rows, BLOCK), jnp.bfloat16)
    weight_flops = 2 * rows * TILE_V * TILE_V

    def cost(blocks, nbytes):
        return pl.CostEstimate(flops=int(blocks * weight_flops), bytes_accessed=nbytes, transcendentals=0)

    first = pl.pallas_call(
        first_kernel, out_shape=packed, in_specs=[VMEM] * 2, out_specs=VMEM, name="first", compiler_params=PARAMS
    )
    center = pl.pallas_call(
        center_kernel, out_shape=state, in_specs=[VMEM] * 2, out_specs=VMEM, name="center",
        compiler_params=PARAMS, cost_estimate=cost(1, 2 << 20),
    )

    def sides(n, *operands):
        return pl.pallas_call(
            functools.partial(sides_kernel, n), out_shape=(state, state), in_specs=[VMEM] * 9, out_specs=(VMEM,) * 2,
            name="sides", input_output_aliases={6: 1}, compiler_params=PARAMS, cost_estimate=cost(1.25, 3 << 20),
        )(*operands)

    update = pl.pallas_call(
        update_kernel, out_shape=(state, packed), in_specs=[VMEM] * 4, out_specs=(VMEM,) * 2,
        name="update", input_output_aliases={2: 0}, compiler_params=PARAMS, cost_estimate=cost(2, 5 << 20),
    )
    scale_row = time_scale[None, :]
    inward_rows = tract_in.transpose(0, 2, 1).reshape(MATCH * rank, TILE_V)

    def advance(n, carry, kicks):
        v, w, both = carry
        inward, outward, weight = [
            pltpu.with_memory_space_constraint(a, pltpu.VMEM) for a in (inward_rows, tract_out, band_weight)
        ]
        own = both[MATCH:]
        far = lax.ppermute(own, "tile", far_route)
        middle = center(both, weight)
        near = swap(both, BASIS[0])
        moving, arrived = both[:MATCH], near[:MATCH]
        for j, mask in enumerate(BASIS[1:]):
            moving = pick(j, arrived, moving)
            arrived = swap(moving, mask)
        base, w = sides(n, odd, near, far, middle, weight, v, w, scale_row, kicks)
        received = pick(len(BASIS) - 1, arrived, moving) * tract_on[0].astype(jnp.bfloat16)[:, None, None]
        v, both = update(received, inward, base, outward)
        return v, w, both

    steps = increments.shape[0]
    unrolled = next(n for n in (5, 2, 1) if steps % n == 0)

    def several(carry, kicks):
        for n in range(unrolled):
            carry = advance(n, carry, kicks)
        return carry, None

    both = first(voltage, tract_out)
    (voltage_end, recovery_end, _), _ = lax.scan(
        several, (voltage, recovery, both), increments.reshape(steps // unrolled, unrolled, rows, TILE_V)
    )
    return voltage_end, recovery_end


def solution(mesh):
    placed = (
        P("real", "tile"),
        P("real", "tile"),
        P(None, "real", "tile"),
        P("tile", None),
        P("tile"),
        P(None, "tile", None),
        P(None, "tile", None),
        P(),
        P("tile", None),
    )
    return jax.shard_map(
        per_device,
        mesh=mesh,
        in_specs=placed,
        out_specs=(P("real", "tile"), P("real", "tile")),
        check_vma=False,
    )
```

```python
import functools
import math

import jax
import jax.numpy as jnp
from jax import lax
from jax.experimental import pallas as pl
from jax.experimental.pallas import tpu as pltpu
from jax.sharding import PartitionSpec as P


TILE_V = 1024
HW = 1024
BLOCK = 256
MATCH = 4
BASIS = (1, 6, 2, 8, 16, 48, 112)

time_step = 0.1
noise_gain = 0.5
shift_a = 0.7
damp_b = 0.8
drive_level = 0.5
band_gain = 1.0
tract_gain = 0.5

HBM = pl.BlockSpec(memory_space=pltpu.HBM)
VMEM = pl.BlockSpec(memory_space=pltpu.VMEM)
PARAMS = pltpu.CompilerParams(vmem_limit_bytes=10 << 20)


def basis_rows(basis, bits):
    rows = [[basis[j] >> i & 1 for j in range(bits)] + [int(i == j) for j in range(bits)] for i in range(bits)]
    for col in range(bits):
        pivot = next(r for r in range(col, bits) if rows[r][col])
        rows[col], rows[pivot] = rows[pivot], rows[col]
        for r in range(bits):
            if r != col and rows[r][col]:
                rows[r] = [a ^ b for a, b in zip(rows[r], rows[col])]
    return [[i for i in range(bits) if rows[j][bits + i]] for j in range(bits)]


def nt(left, right):
    return lax.dot_general(left, right, (((1,), (1,)), ((), ())), preferred_element_type=jnp.float32)


def project(vb, tract_out_ref, packed_ref):
    for m in range(MATCH):
        packed_ref[m] = jnp.dot(vb, tract_out_ref[m], preferred_element_type=jnp.float32).astype(jnp.bfloat16)


def first_kernel(v_hbm, w_hbm, tract_out_hbm, v_out, w_out, packed_ref, tract_out_ref, sems):
    copies = [pltpu.make_async_copy(v_hbm, v_out, sems.at[MATCH]), pltpu.make_async_copy(w_hbm, w_out, sems.at[MATCH + 1])]
    copies += [pltpu.make_async_copy(tract_out_hbm.at[m], tract_out_ref.at[m], sems.at[m]) for m in range(MATCH)]
    for copy in copies:
        copy.start()
    copies[0].wait()
    vb = v_out[...].astype(jnp.bfloat16)
    for j in range(HW // BLOCK):
        packed_ref[MATCH + j] = vb[:, j * BLOCK : (j + 1) * BLOCK]
    for m in range(MATCH):
        copies[2 + m].wait()
        packed_ref[m] = jnp.dot(vb, tract_out_ref[m], preferred_element_type=jnp.float32).astype(jnp.bfloat16)
    copies[1].wait()


def center_kernel(packed_ref, weight_ref, out_ref):
    vb = jnp.concatenate([packed_ref[MATCH + j] for j in range(TILE_V // BLOCK)], axis=1)
    for i in range(TILE_V // BLOCK):
        rows = slice(i * BLOCK, (i + 1) * BLOCK)
        out_ref[:, rows] = nt(vb, weight_ref[rows, HW : HW + TILE_V])


def center_loading_kernel(packed_ref, weight_hbm, out_ref, part_ref, sems):
    copies = []
    for i in range(TILE_V // BLOCK):
        rows = pl.ds(i * BLOCK, BLOCK)
        copies.append(
            pltpu.make_async_copy(weight_hbm.at[rows, pl.ds(HW, TILE_V)], part_ref.at[rows], sems.at[i])
        )
        copies[i].start()
    vb = jnp.concatenate([packed_ref[MATCH + j] for j in range(TILE_V // BLOCK)], axis=1)
    for i in range(TILE_V // BLOCK):
        rows = slice(i * BLOCK, (i + 1) * BLOCK)
        copies[i].wait()
        out_ref[:, rows] = nt(vb, part_ref[rows, :])


def sides_kernel(
    n, odd_ref, near_ref, far_ref, center_ref, weight_ref, v_ref, w_ref, scale_ref, kick_ref, base_ref, w_out
):
    odd = odd_ref[...] > 0.5
    left, right = [], []
    for j in range(HW // BLOCK):
        near, far = near_ref[MATCH + j].astype(jnp.float32), far_ref[j].astype(jnp.float32)
        left.append(jnp.where(odd, near, far).astype(jnp.bfloat16))
        right.append(jnp.where(odd, far, near).astype(jnp.bfloat16))
    row = lax.broadcasted_iota(jnp.int32, (BLOCK, BLOCK), 0)
    col = lax.broadcasted_iota(jnp.int32, (BLOCK, BLOCK), 1)

    def weights(i, column, keep=None):
        block = weight_ref[i * BLOCK : (i + 1) * BLOCK, column : column + BLOCK]
        if keep is None:
            return block
        return jnp.where(keep, block.astype(jnp.float32), 0.0).astype(jnp.bfloat16)

    for i in range(TILE_V // BLOCK):
        cols = slice(i * BLOCK, (i + 1) * BLOCK)
        band = center_ref[:, cols]
        for j in range(i, HW // BLOCK):
            band += nt(left[j], weights(i, j * BLOCK, col >= row if j == i else None))
        for j in range(i + 1):
            band += nt(right[j], weights(i, HW + TILE_V + j * BLOCK, col <= row if j == i else None))
        v, w = v_ref[:, cols], w_ref[:, cols]
        rate = v - v * v * v / 3.0 - w + band_gain * band + drive_level
        base_ref[:, cols] = v + time_step * rate + noise_gain * math.sqrt(time_step) * kick_ref[n, :, cols]
        w_out[:, cols] = w + time_step * scale_ref[:, cols] * (v + shift_a - damp_b * w)


def update_kernel(received_ref, tract_in_ref, base_ref, tract_out_ref, v_out, packed_ref):
    rounded = []
    for i in range(TILE_V // BLOCK):
        cols = slice(i * BLOCK, (i + 1) * BLOCK)
        tract = nt(received_ref[0], tract_in_ref[0, cols, :])
        for m in range(1, MATCH):
            tract += nt(received_ref[m], tract_in_ref[m, cols, :])
        v_new = base_ref[:, cols] + time_step * tract_gain * tract
        v_out[:, cols] = v_new
        rounded.append(v_new.astype(jnp.bfloat16))
        packed_ref[MATCH + i] = rounded[i]
    project(jnp.concatenate(rounded, axis=1), tract_out_ref, packed_ref)


def per_device(
    voltage, recovery, increments, band_weight, time_scale, tract_in, tract_out, matching_masks, tract_on
):
    count = lax.axis_size("tile")
    bits = count.bit_length() - 1
    rows = voltage.shape[0]
    parities = basis_rows(BASIS, bits)
    odd = jnp.full((rows, BLOCK), jnp.bitwise_and(lax.axis_index("tile"), 1), jnp.float32)
    far_route = [(i, i + 1) for i in range(1, count - 1, 2)] + [(i + 1, i) for i in range(1, count - 1, 2)]

    def pick(j, arrived, kept):
        folded = sum(jnp.right_shift(matching_masks, b) for b in parities[j])
        chosen = jnp.bitwise_and(folded, 1) == 1
        return jnp.where(chosen[:, None, None], arrived, kept)

    def swap(block, mask):
        return lax.ppermute(block, "tile", [(i, i ^ mask) for i in range(count)])

    state = jax.ShapeDtypeStruct(voltage.shape, jnp.float32)
    packed = jax.ShapeDtypeStruct((MATCH + HW // BLOCK, rows, BLOCK), jnp.bfloat16)
    weight_flops = 2 * rows * TILE_V * TILE_V

    def cost(blocks, nbytes):
        return pl.CostEstimate(flops=int(blocks * weight_flops), bytes_accessed=nbytes, transcendentals=0)

    first = pl.pallas_call(
        first_kernel, out_shape=(state, state, packed), in_specs=[HBM] * 3, out_specs=(VMEM,) * 3, name="first",
        compiler_params=PARAMS,
        scratch_shapes=[pltpu.VMEM(tract_out.shape, tract_out.dtype), pltpu.SemaphoreType.DMA((MATCH + 2,))],
    )
    center = pl.pallas_call(
        center_kernel, out_shape=state, in_specs=[VMEM] * 2, out_specs=VMEM, name="center",
        compiler_params=PARAMS, cost_estimate=cost(1, 2 << 20),
    )

    center_loading = pl.pallas_call(
        center_loading_kernel, out_shape=state, in_specs=[VMEM, HBM], out_specs=VMEM, name="center",
        compiler_params=PARAMS, cost_estimate=cost(1, 2 << 20),
        scratch_shapes=[pltpu.VMEM((TILE_V, TILE_V), jnp.bfloat16), pltpu.SemaphoreType.DMA((TILE_V // BLOCK,))],
    )
    stored = pltpu.with_memory_space_constraint(band_weight, pltpu.HBM)

    def sides(n, *operands):
        return pl.pallas_call(
            functools.partial(sides_kernel, n), out_shape=(state, state), in_specs=[VMEM] * 9, out_specs=(VMEM,) * 2,
            name="sides", input_output_aliases={6: 1}, compiler_params=PARAMS, cost_estimate=cost(1.25, 3 << 20),
        )(*operands)

    update = pl.pallas_call(
        update_kernel, out_shape=(state, packed), in_specs=[VMEM] * 4, out_specs=(VMEM,) * 2,
        name="update", input_output_aliases={2: 0}, compiler_params=PARAMS, cost_estimate=cost(2, 5 << 20),
    )
    scale_row = time_scale[None, :]

    def advance(n, carry, kicks):
        v, w, both = carry
        inward, outward, weight = [
            pltpu.with_memory_space_constraint(a, pltpu.VMEM) for a in (tract_in, tract_out, band_weight)
        ]
        own = both[MATCH:]
        far = lax.ppermute(own, "tile", far_route)
        middle = center(both, weight) if n else center_loading(both, stored)
        near = swap(both, BASIS[0])
        moving, arrived = both[:MATCH], near[:MATCH]
        for j, mask in enumerate(BASIS[1:]):
            moving = pick(j, arrived, moving)
            arrived = swap(moving, mask)
        base, w = sides(n, odd, near, far, middle, weight, v, w, scale_row, kicks)
        received = pick(len(BASIS) - 1, arrived, moving)
        received = jnp.where((tract_on[0] == 1)[:, None, None], received, jnp.zeros_like(received))
        v, both = update(received, inward, base, outward)
        return v, w, both

    steps = increments.shape[0]
    unrolled = next(n for n in (5, 2, 1) if steps % n == 0)
    trips = increments.reshape(steps // unrolled, unrolled, rows, TILE_V)

    def several(carry):
        trip, *rest = carry
        kicks = lax.dynamic_index_in_dim(trips, trip, 0, keepdims=False, allow_negative_indices=False)
        for n in range(unrolled):
            rest = advance(n, rest, kicks)
        trip, *rest = lax.optimization_barrier((trip, *rest))
        return trip + 1, *rest

    v, w, both = first(*[pltpu.with_memory_space_constraint(a, pltpu.HBM) for a in (voltage, recovery, tract_out)])
    _, voltage_end, recovery_end, _ = lax.while_loop(
        lambda carry: carry[0] < steps // unrolled, several, (jnp.int32(0), v, w, both)
    )
    return voltage_end, recovery_end


def solution(mesh):
    placed = (
        P("real", "tile"),
        P("real", "tile"),
        P(None, "real", "tile"),
        P("tile", None),
        P("tile"),
        P(None, "tile", None),
        P(None, "tile", None),
        P(),
        P("tile", None),
    )
    return jax.shard_map(
        per_device,
        mesh=mesh,
        in_specs=placed,
        out_specs=(P("real", "tile"), P("real", "tile")),
        check_vma=False,
    )
```
